256 devices in a mesh: freq: 128 (over x, y, z_hi, core), plane: 2 (over z_lo).
Axes of the slice: x: 4, y: 4, z: 8 (z_hi: 4, z_lo: 2; z = z_hi * 2 + z_lo), core: 2. Of those that a mesh axis runs over, the one named last changes fastest.
Arguments:
- state_in: float32 [2, 256, 5, 256, 128], P(None, 'freq', None, 'plane'), may hold values from -6 to 6
- forcing_in: float32 [2, 256, 5, 256, 128], P(None, 'freq', None, 'plane'), may hold values from -6 to 6
- base_flow: float32 [128, 5, 256, 128], P('freq', None, 'plane'), may hold values from -1 to 1
- station_index: int32 [2], replicated, may hold values from 0 to 127
- lobe_count: int32 [1], replicated, may hold values from 3 to 127
Outputs:
- state_out: float32 [2, 256, 5, 256, 128], P(None, 'freq', None, 'plane')
- forcing_out: float32 [2, 256, 5, 256, 128], P(None, 'freq', None, 'plane')
The draws below stay inside these ranges and needn't reach their ends.
All inputs are finite; a program needn't handle non-finite values.
Results may differ from the reference program's by a relative error of at most 0.0003.
Values sent between devices are 32-bit elements; how exact they have to be, the bound alone decides.
No kernel may reach another device: no remote copies, remote signals or barrier semaphores. Data moves between devices by JAX's collectives and lax.ppermute only.
A program may use at most 128 MiB of HBM per device.

```python
import math
import jax
import jax.numpy as jnp
from jax import lax

VARS = 5
R = 128
A = 256
SWEEPS = 4
STEPS = 2
F = 256
NT = 384
STATIONS = 128


def block_levels(stream_key, dims, split, smallest, largest):
    gain, own = 1.0, jax.random.fold_in(stream_key, 6)
    for dim, parts in split:
        heights = jnp.exp(jax.random.uniform(jax.random.fold_in(own, dim), (parts,), jnp.float32, smallest / len(split), largest / len(split)))
        gain = gain * jnp.repeat(heights, dims[dim] // parts).reshape([-1 if axis == dim else 1 for axis in range(len(dims))])
    return gain


def noise(own_key, dims, scale, bound, shards=(), held_as=jnp.bfloat16):
    array = jax.random.normal(own_key, dims, jnp.float32) * scale
    if len(shards) > 0:
        array = block_levels(own_key, dims, shards, -0.22, 0.18) * array
    return jnp.clip(array, min=-bound, max=bound).astype(held_as)


def setup_inputs(seed: int = 0) -> dict:
    streams_of = jax.random.split(jax.random.key(seed), 6)
    state_in = noise(streams_of[0], (2, F, VARS, A, R), 1.0, 6.0, ((1, 128), (3, 2)), jnp.float32)
    forcing_in = noise(streams_of[1], (2, F, VARS, A, R), 1.0, 6.0, ((1, 128), (3, 2)), jnp.float32)
    base_flow = jnp.clip(jax.random.uniform(streams_of[2], (STATIONS, VARS, A, R), jnp.float32, -1.0, 1.0) * block_levels(streams_of[2], (STATIONS, VARS, A, R), ((0, 128), (2, 2)), -0.4, 0.0), -1.0, 1.0)
    station_index = jax.random.randint(streams_of[3], (STEPS,), 0, STATIONS).astype(jnp.int32)
    lobe_count = jax.random.randint(streams_of[4], (1,), 3, 128).astype(jnp.int32)
    return {"state_in": state_in, "forcing_in": forcing_in, "base_flow": base_flow, "station_index": station_index, "lobe_count": lobe_count}


SIDE_WEIGHT = 1.25
MARCH_WEIGHT = 4.0
DIAG_SHIFT = 4.0
ADVECT_SCALE = 0.5
BASE_SCALE = 0.5
HIGHEST_MODE = lax.Precision.HIGHEST

def radial_tables(radius_count):
    indices = jnp.arange(radius_count)
    angles = math.pi * indices.astype(jnp.float32) / (radius_count - 1)
    cheb_nodes = jnp.cos(angles)
    weights = jnp.where((indices == 0) | (indices == radius_count - 1), 2.0, 1.0).astype(jnp.float32)
    parity = (1 - 2 * ((indices[:, None] + indices[None, :]) % 2)).astype(jnp.float32)
    offdiag = indices[:, None] != indices[None, :]
    spacing = jnp.where(offdiag, cheb_nodes[:, None] - cheb_nodes[None, :], 1.0)
    entries = jnp.where(offdiag, weights[:, None] / weights[None, :] * parity / spacing, 0.0)
    entries = entries - jnp.diag(lax.optimization_barrier(jnp.sum(entries, axis=1)))
    slopes = jnp.sin(angles)[:, None] * entries / (radius_count - 1)
    stiffness = jnp.dot(slopes.T, slopes, precision=HIGHEST_MODE)
    system = stiffness + DIAG_SHIFT * jnp.eye(radius_count, dtype=jnp.float32)
    factor = jnp.linalg.cholesky(system)
    factor_inv = lax.linalg.triangular_solve(factor, jnp.eye(radius_count, dtype=jnp.float32), left_side=True, lower=True)
    return (slopes, jnp.dot(factor_inv.T, factor_inv, precision=HIGHEST_MODE))

def transform_tables(freqs, ntime):
    mode_ids = jnp.arange(freqs)
    time_ids = jnp.arange(ntime)
    phases = mode_ids[:, None] * time_ids[None, :] % ntime
    angles = 2.0 * math.pi * phases.astype(jnp.float32) / ntime
    cosines = jnp.cos(angles)
    sine_tab = jnp.sin(angles)
    stacked = jnp.concatenate([cosines, -sine_tab], axis=0)
    return (stacked.T / math.sqrt(freqs), stacked / math.sqrt(ntime))

def chevron(lobe_count, azimuths, start_az, total_az):
    position = (start_az + jnp.arange(azimuths)).astype(jnp.int32)
    phases = lobe_count[0] * position % total_az
    return 1.0 + 0.5 * jnp.cos(2.0 * math.pi * phases.astype(jnp.float32) / total_az)

def relax_sweep(inner, neighbours, right_side, coefficient, omegas, inverse_p):
    real_part = inner[0]
    imag_part = inner[1]
    rate_col = omegas[:, None, None, None]
    scaled = coefficient[None]
    mixing = jnp.stack([scaled * real_part - rate_col * imag_part, scaled * imag_part + rate_col * real_part])
    summed = right_side - mixing + SIDE_WEIGHT * neighbours
    radius_count = summed.shape[-1]
    return jnp.dot(summed.reshape(-1, radius_count), inverse_p.T, precision=HIGHEST_MODE).reshape(summed.shape)

def advect(velocity, radial_time, around_time):
    carried = velocity[:, 1:2] * radial_time + velocity[:, 2:3] * around_time
    spread = velocity[:, 0] * (radial_time[:, 1] + around_time[:, 2])
    carried = jnp.concatenate([carried[:, 0:1] + spread[:, None], carried[:, 1:]], axis=1)
    return -ADVECT_SCALE * carried

def forcing_of(march_state, slopes, inverse, forward):
    radial = jnp.dot(march_state.reshape(-1, R), slopes.T, precision=HIGHEST_MODE).reshape(march_state.shape)
    beside_all = 0.5 * (jnp.roll(march_state, -1, 3) - jnp.roll(march_state, 1, 3))
    fields = jnp.stack([march_state, radial, beside_all])
    az_block = 32 if A % 32 == 0 else A
    pieces = []
    for first_az in range(0, A, az_block):
        block_data = fields[:, :, :, :, first_az:first_az + az_block, :].reshape(3, 2 * F, -1)
        in_time = jnp.einsum('tc,kcx->ktx', inverse, block_data, precision=HIGHEST_MODE).reshape(3, NT, VARS, -1)
        source = advect(in_time[0], in_time[1], in_time[2])
        spectral = jnp.dot(forward, source.reshape(NT, -1), precision=HIGHEST_MODE)
        pieces.append(spectral.reshape(2, F, VARS, az_block, R))
    return jnp.concatenate(pieces, axis=3)

def reference(state_in, forcing_in, base_flow, station_index, lobe_count):
    slopes, inverse_p = radial_tables(R)
    inverse, forward = transform_tables(F, NT)
    omegas = 0.5 * jnp.arange(F).astype(jnp.float32) / F
    shape_az = chevron(lobe_count, A, 0, A)
    march_state = state_in
    forcing = forcing_in
    for station in range(STEPS):
        plane_flow = lax.dynamic_index_in_dim(base_flow, station_index[station], 0, keepdims=False)
        coefficient = BASE_SCALE * plane_flow * shape_az[None, :, None]
        right_side = MARCH_WEIGHT * march_state + forcing
        iterate = march_state
        for sweep_no in range(SWEEPS):
            iterate = relax_sweep(iterate, jnp.roll(iterate, -1, 3) + jnp.roll(iterate, 1, 3), right_side, coefficient, omegas, inverse_p)
        march_state = iterate
        forcing = forcing_of(march_state, slopes, inverse, forward)
    return (march_state, forcing)
```

```python
import itertools
import math

import jax
import jax.numpy as jnp
import numpy as np
from jax import lax
from jax.experimental import pallas as pl
from jax.experimental.pallas import tpu as pltpu
from jax.sharding import PartitionSpec as P

SWEEPS = 4
STEPS = 2
SIDE_WEIGHT = 1.25
MARCH_WEIGHT = 4.0
DIAG_SHIFT = 4.0
ADVECT_SCALE = 0.5
BASE_SCALE = 0.5

NF = 128
PER = 2
NV = 5
AZ = 128
ALL_AZ = 256
R = 128
FREQS = NF * PER
NT = 3 * FREQS // 2
NC = 2 * PER * NV
HALO = 8
EXT = AZ + 2 * HALO
GUARD = 8
SLICE = 24


def freq_index(x, y, z, c):
    return ((x * 4 + y) * 4 + z) * 2 + c


def ring_orders():
    snake = [
        (x, y) for y in range(4) for x in (range(4) if y % 2 == 0 else range(3, -1, -1))
    ]
    cycle = [(0, 0), (1, 0), (2, 0), (3, 0), (3, 1), (3, 2), (3, 3), (2, 3)]
    cycle += [(2, 2), (2, 1), (1, 1), (1, 2), (1, 3), (0, 3), (0, 2), (0, 1)]

    def walk(start, end):
        i = cycle.index(start)
        forward = cycle[i:] + cycle[:i]
        if forward[-1] == end:
            return forward
        return [cycle[i]] + cycle[:i][::-1] + cycle[i + 1 :][::-1]

    first = []
    for z in range(4):
        first += [(x, y, z) for x, y in (snake if z % 2 == 0 else snake[::-1])]
    second = [(y, x, 3) for x, y in snake]
    second += [(x, y, 2) for x, y in walk((3, 0), (2, 0))]
    second += [(x, y, 1) for x, y in walk((2, 0), (1, 0))]
    second += [(x, y, 0) for x, y in walk((1, 0), (0, 0))]
    return [
        [freq_index(x, y, z, c) for x, y, z in path for c in (0, 1)]
        for path in (first, second)
    ]


ORDERS = ring_orders()
AZ_OF = np.argsort(np.array(ORDERS), axis=1).astype(np.int32)
RING = [f * 2 + p for p in (0, 1) for f in ORDERS[p]]
TO_NEXT = [(RING[i], RING[(i + 1) % ALL_AZ]) for i in range(ALL_AZ)]
TO_PREV = [(RING[(i + 1) % ALL_AZ], RING[i]) for i in range(ALL_AZ)]
SHEETS = [
    [freq_index(x, y, z, c) for x, y, c in itertools.product(range(4), range(4), range(2))]
    for z in range(4)
]


def z_shift(step):
    return [
        (freq_index(x, y, z, c), freq_index(x, y, (z + step) % 4, c))
        for x, y, z, c in itertools.product(range(4), range(4), range(4), range(2))
    ]


def split(table):
    table = np.asarray(table, np.float32)
    high = table.astype(jnp.bfloat16)
    low = (table - high.astype(np.float32)).astype(jnp.bfloat16)
    return high, low


def radial_tables():
    j = np.arange(R)
    phi = math.pi * j / (R - 1)
    x = np.cos(phi)
    c = np.where((j == 0) | (j == R - 1), 2.0, 1.0)
    parity = 1.0 - 2.0 * ((j[:, None] + j[None, :]) % 2)
    off = j[:, None] != j[None, :]
    gap = -2.0 * np.sin((phi[:, None] + phi[None, :]) / 2) * np.sin(
        (phi[:, None] - phi[None, :]) / 2
    )
    entries = np.where(off, c[:, None] / c[None, :] * parity / np.where(off, gap, 1.0), 0.0)
    entries = entries - np.diag(entries.sum(axis=1))
    slopes = np.sin(phi)[:, None] * entries / (R - 1)
    inverse = np.linalg.inv(slopes.T @ slopes + DIAG_SHIFT * np.eye(R))
    return slopes, inverse


def right_factor(matrix):
    high, low = split(np.asarray(matrix).T)
    half = np.concatenate([high, low], axis=1)
    return np.concatenate([half, half], axis=0)


def transform_tables():
    k = np.arange(FREQS)
    n = np.arange(NT)
    angle = 2.0 * math.pi * ((k[:, None] * n[None, :]) % NT) / NT
    table = np.stack([np.cos(angle), -np.sin(angle)])
    table = table.reshape(2, NF, PER, NT).transpose(1, 0, 2, 3).reshape(2 * FREQS, NT)
    inverse = np.concatenate(split(table.T / math.sqrt(FREQS)), axis=0)
    forward = np.concatenate(split(table / math.sqrt(NT)), axis=0)
    return inverse, forward


def halves(t):
    high = t.astype(jnp.bfloat16)
    low = (t - high.astype(jnp.float32)).astype(jnp.bfloat16)
    return jnp.concatenate([high, low], axis=1)


def along_radii(t, factor):
    both = jnp.dot(halves(t), factor, preferred_element_type=jnp.float32)
    return both[:, :R] + both[:, R:]


def transformed(table, t, rows):
    quad = jnp.dot(table, halves(t), preferred_element_type=jnp.float32)
    return (quad[:rows, :R] + quad[rows:, :R]) + (quad[:rows, R:] + quad[rows:, R:])


def march_kernel(last, *refs):
    if last:
        az_ref, om_ref, ext_ref, force_ref, fedge_ref, w_ref, q_ref = refs[:7]
        outs = refs[7:]
    else:
        az_ref, om_ref, state_ref, sedge_ref, force_ref, fedge_ref, w_ref, q_ref = refs[:8]
        outs = refs[8:]
    keep_ref, send_ref, it_ref, b_ref = outs
    for c in range(NC):
        at = GUARD + c * EXT
        own = pl.ds(c * AZ, AZ)
        head = pl.ds(c * 2 * HALO, HALO)
        tail = pl.ds(c * 2 * HALO + HALO, HALO)
        if last:
            it_ref[0, pl.ds(at, EXT), :] = ext_ref[pl.ds(c * EXT, EXT), :]
        else:
            it_ref[0, pl.ds(at, HALO), :] = sedge_ref[tail, :]
            it_ref[0, pl.ds(at + HALO, AZ), :] = state_ref[own, :]
            it_ref[0, pl.ds(at + HALO + AZ, HALO), :] = sedge_ref[head, :]
        for lo, size, part, ref in (
            (0, HALO, tail, fedge_ref),
            (HALO, AZ, own, force_ref),
            (HALO + AZ, HALO, head, fedge_ref),
        ):
            b_ref[pl.ds(c * EXT + lo, size), :] = (
                MARCH_WEIGHT * it_ref[0, pl.ds(at + lo, size), :] + ref[part, :]
            )

    factor = q_ref[...]

    def sweep(step, carry):
        now = lax.rem(step, 2)
        new = 1 - now
        for v in range(NV):
            w = w_ref[pl.ds(v * EXT, EXT), :]
            terms = [None] * 4
            for j in range(PER):
                rate = om_ref[j]
                planes = (j * NV + v, (PER + j) * NV + v)
                re, im = (it_ref[now, pl.ds(GUARD + c * EXT, EXT), :] for c in planes)
                for part, (c, mixed) in enumerate(
                    ((planes[0], w * re - rate * im), (planes[1], w * im + rate * re))
                ):
                    beside = (
                        it_ref[now, pl.ds(GUARD + c * EXT + 1, EXT), :]
                        + it_ref[now, pl.ds(GUARD + c * EXT - 1, EXT), :]
                    )
                    terms[part * PER + j] = (
                        b_ref[pl.ds(c * EXT, EXT), :] - mixed + SIDE_WEIGHT * beside
                    )
            done = along_radii(jnp.concatenate(terms, axis=0), factor)
            for i in range(4):
                it_ref[new, pl.ds(GUARD + (i * NV + v) * EXT, EXT), :] = done[
                    i * EXT : (i + 1) * EXT
                ]
        return carry

    lax.fori_loop(0, SWEEPS, sweep, 0)
    for c in range(NC):
        at = GUARD + c * EXT
        if last:
            keep_ref[pl.ds(c * AZ, AZ), :] = it_ref[0, pl.ds(at + HALO, AZ), :]
        else:
            keep_ref[pl.ds(c * EXT, EXT), :] = it_ref[0, pl.ds(at, EXT), :]
    final = it_ref.at[0]
    for f in range(NF):
        send_ref[pl.ds(f * NC, NC), :] = final[
            pl.ds(GUARD + HALO + az_ref[f], NC, stride=EXT), :
        ]


def to_time_kernel(points_ref, table_ref, u_ref):
    table = table_ref[...]

    def one(v, carry):
        x = points_ref[pl.ds(v, 2 * FREQS, stride=NV), :]
        u_ref[pl.ds(pl.multiple_of(v * NT, NT), NT), :] = transformed(table, x, NT)
        return carry

    lax.fori_loop(0, NV, one, 0)


def radial_kernel(u_ref, slope_ref, out_ref):
    factor = slope_ref[...]
    u0, u1 = u_ref[pl.ds(0, NT), :], u_ref[pl.ds(NT, NT), :]
    for v in (1, 0, 2, 3, 4):
        ur = along_radii(u_ref[pl.ds(v * NT, NT), :], factor)
        if v == 1:
            spread = u0 * ur
        carried = u1 * ur
        if v == 0:
            carried = carried + spread
        out_ref[pl.ds(v * NT, NT), :] = -ADVECT_SCALE * carried


def to_freq_kernel(u_ref, part_ref, next_ref, prev_ref, table_ref, out_ref):
    table = table_ref[...]
    u2 = u_ref[pl.ds(2 * NT, NT), :]

    def around(v):
        rows = pl.ds(pl.multiple_of(v * NT, NT), NT)
        return 0.5 * (next_ref[rows, :] - prev_ref[rows, :])

    def one(v, carry):
        rows = pl.ds(pl.multiple_of(v * NT, NT), NT)
        n = part_ref[rows, :] - ADVECT_SCALE * (u2 * around(v))
        extra = jnp.where(v == 0, ADVECT_SCALE, 0.0)
        n = n - extra * (u_ref[pl.ds(0, NT), :] * around(2))
        out_ref[pl.ds(v, 2 * FREQS, stride=NV), :] = transformed(table, n, 2 * FREQS)
        return carry

    lax.fori_loop(0, NV, one, 0)


def place_kernel(az_ref, got_ref, out_ref):
    for f in range(NF):
        out_ref[pl.ds(az_ref[f], NC, stride=AZ), :] = got_ref[pl.ds(f * NC, NC), :]


VMEM = pl.BlockSpec(memory_space=pltpu.VMEM)
SMEM = pl.BlockSpec(memory_space=pltpu.SMEM)


def call(kernel, specs, rows, name, flops, scratch=()):
    shapes = [jax.ShapeDtypeStruct((n, R), jnp.float32) for n in rows]
    return pl.pallas_call(
        kernel,
        in_specs=specs,
        out_specs=[VMEM] * len(rows) if len(rows) > 1 else VMEM,
        out_shape=shapes if len(rows) > 1 else shapes[0],
        scratch_shapes=list(scratch),
        compiler_params=pltpu.CompilerParams(vmem_limit_bytes=40 << 20),
        cost_estimate=pl.CostEstimate(
            flops=flops, bytes_accessed=4 * NC * AZ * R * 4, transcendentals=0
        ),
        name=name,
    )


def exchange(blocks):
    return lax.all_to_all(
        blocks.reshape(NF, NV, 4, R), "freq", split_axis=0, concat_axis=0, tiled=True
    ).reshape(NF * NC, R)


def edges(planes):
    count = planes.shape[0] // AZ
    planes = planes.reshape(count, AZ, R)
    mine = jnp.concatenate([planes[:, :HALO], planes[:, AZ - HALO :]], axis=1)
    return lax.ppermute(mine.reshape(-1, R), "plane", [(0, 1), (1, 0)])


def fetch_planes(base_flow, station_index):
    plane = base_flow.reshape(NV, AZ, R)
    beside = edges(plane.reshape(-1, R)).reshape(NV, 2 * HALO, R)
    whole = jnp.concatenate([beside[:, HALO:], plane, beside[:, :HALO]], axis=1)
    whole = whole.reshape(-1, R)
    whole = jnp.pad(whole, ((0, 32 * SLICE - whole.shape[0]), (0, 0)))
    held = lax.all_to_all(
        whole.reshape(32, SLICE, R),
        "freq",
        split_axis=0,
        concat_axis=0,
        tiled=True,
        axis_index_groups=SHEETS,
    )
    sheet = (station_index // 8) * 2 + station_index % 2
    mine = jnp.concatenate(
        [lax.dynamic_slice_in_dim(held, sheet[s], 1, axis=0) for s in range(STEPS)], axis=0
    )
    my_z = (lax.axis_index("freq") // 2) % 4
    behind = (my_z - station_index // 2) % 4
    chosen = mine
    for step in (1, 2, 3):
        came = lax.ppermute(mine, "freq", z_shift(step))
        chosen = jnp.where((behind == step)[:, None, None], came, chosen)
    spread = lax.all_to_all(
        jnp.broadcast_to(chosen[None], (32, STEPS, SLICE, R)),
        "freq",
        split_axis=0,
        concat_axis=0,
        tiled=True,
        axis_index_groups=SHEETS,
    )
    return [spread[:, s].reshape(-1, R)[: NV * EXT] for s in range(STEPS)]


def per_device(state_in, forcing_in, base_flow, station_index, lobe_count):
    slopes, inverse_p = radial_tables()
    solve = jnp.asarray(right_factor(inverse_p))
    slope = jnp.asarray(right_factor(slopes))
    inverse, forward = (jnp.asarray(t) for t in transform_tables())
    f = lax.axis_index("freq")
    p = lax.axis_index("plane")
    az_of = jnp.where(p == 0, jnp.asarray(AZ_OF[0]), jnp.asarray(AZ_OF[1]))
    omegas = 0.5 * (f * PER + jnp.arange(PER)).astype(jnp.float32) / FREQS
    position = (p * AZ - HALO + jnp.arange(EXT) + ALL_AZ) % ALL_AZ
    phases = lobe_count[0] * position % ALL_AZ
    shape_az = 1.0 + 0.5 * jnp.cos(2.0 * math.pi * phases.astype(jnp.float32) / ALL_AZ)
    shape_az = jnp.tile(shape_az, NV)[:, None]

    march = NC * AZ * R
    scratch = (
        pltpu.VMEM((2, NC * EXT + 2 * GUARD, R), jnp.float32),
        pltpu.VMEM((NC * EXT, R), jnp.float32),
    )
    state = state_in.reshape(NC * AZ, R)
    forcing = forcing_in.reshape(NC * AZ, R)
    state_edges = edges(state)
    planes = fetch_planes(base_flow, station_index)
    for station in range(STEPS):
        last = station == STEPS - 1
        weight = BASE_SCALE * planes[station] * shape_az
        forcing_edges = edges(forcing)
        start = (state,) if last else (state, state_edges)
        state, send = call(
            lambda *refs, last=last: march_kernel(last, *refs),
            [SMEM, SMEM] + [VMEM] * (len(start) + 4),
            (NC * (AZ if last else EXT), NC * AZ),
            "march",
            march * 2048,
            scratch,
        )(az_of, omegas, *start, forcing, forcing_edges, weight, solve)
        points = exchange(send)
        u = call(to_time_kernel, [VMEM] * 2, (NV * NT,), "to_time", march * 3072)(
            points, inverse
        )
        ahead = lax.ppermute(u, ("freq", "plane"), TO_PREV)
        behind = lax.ppermute(u, ("freq", "plane"), TO_NEXT)
        part = call(radial_kernel, [VMEM] * 2, (NV * NT,), "radial", march * 768)(u, slope)
        back = call(to_freq_kernel, [VMEM] * 5, (NC * AZ,), "to_freq", march * 3072)(
            u, part, ahead, behind, forward
        )
        got = exchange(back)
        forcing = call(place_kernel, [SMEM, VMEM], (NC * AZ,), "place", march)(az_of, got)
    return (state.reshape(state_in.shape), forcing.reshape(state_in.shape))


def solution(mesh):
    return jax.shard_map(
        per_device,
        mesh=mesh,
        in_specs=(
            P(None, "freq", None, "plane", None),
            P(None, "freq", None, "plane", None),
            P("freq", None, "plane", None),
            P(),
            P(),
        ),
        out_specs=(P(None, "freq", None, "plane", None), P(None, "freq", None, "plane", None)),
        check_vma=False,
    )
```

```python
import itertools
import math

import jax
import jax.numpy as jnp
import numpy as np
from jax import lax
from jax.experimental import pallas as pl
from jax.experimental.pallas import tpu as pltpu
from jax.sharding import PartitionSpec as P

SWEEPS = 4
STEPS = 2
SIDE_WEIGHT = 1.25
MARCH_WEIGHT = 4.0
DIAG_SHIFT = 4.0
ADVECT_SCALE = 0.5
BASE_SCALE = 0.5

NF = 128
PER = 2
NV = 5
AZ = 128
ALL_AZ = 256
R = 128
FREQS = NF * PER
NT = 3 * FREQS // 2
NC = 2 * PER * NV
HALO = 8
EXT = AZ + 2 * HALO
GUARD = 8
KEPT = 2 * FREQS
CHUNKS = ((0, 1, 2), (3, 4))
COST = 1e8


def freq_index(x, y, z, c):
    return ((x * 4 + y) * 4 + z) * 2 + c


def ring_orders():
    snake = [
        (x, y) for y in range(4) for x in (range(4) if y % 2 == 0 else range(3, -1, -1))
    ]
    cycle = [(0, 0), (1, 0), (2, 0), (3, 0), (3, 1), (3, 2), (3, 3), (2, 3)]
    cycle += [(2, 2), (2, 1), (1, 1), (1, 2), (1, 3), (0, 3), (0, 2), (0, 1)]

    def walk(start, end):
        i = cycle.index(start)
        forward = cycle[i:] + cycle[:i]
        if forward[-1] == end:
            return forward
        return [cycle[i]] + cycle[:i][::-1] + cycle[i + 1 :][::-1]

    first = []
    for z in range(4):
        first += [(x, y, z) for x, y in (snake if z % 2 == 0 else snake[::-1])]
    second = [(y, x, 3) for x, y in snake]
    second += [(x, y, 2) for x, y in walk((3, 0), (2, 0))]
    second += [(x, y, 1) for x, y in walk((2, 0), (1, 0))]
    second += [(x, y, 0) for x, y in walk((1, 0), (0, 0))]
    return [
        [freq_index(x, y, z, c) for x, y, z in path for c in (0, 1)]
        for path in (first, second)
    ]


ORDERS = ring_orders()
AZ_OF = np.argsort(np.array(ORDERS), axis=1).astype(np.int32)
RING = [f * 2 + p for p in (0, 1) for f in ORDERS[p]]
TO_NEXT = [(RING[i], RING[(i + 1) % ALL_AZ]) for i in range(ALL_AZ)]
TO_PREV = [(RING[(i + 1) % ALL_AZ], RING[i]) for i in range(ALL_AZ)]
FLAT = [[g * 8 + s for g in range(16)] for s in range(8)]
TALL = [[g * 8 + s for s in range(8)] for g in range(16)]
EDGE_AT = np.array(
    [[ORDERS[p][a] for a in (*range(HALO), *range(AZ - HALO, AZ))] for p in (0, 1)], np.int32
)


def split(table):
    table = np.asarray(table, np.float32)
    high = table.astype(jnp.bfloat16)
    low = (table - high.astype(np.float32)).astype(jnp.bfloat16)
    return high, low


def radial_tables():
    j = np.arange(R)
    phi = math.pi * j / (R - 1)
    x = np.cos(phi)
    c = np.where((j == 0) | (j == R - 1), 2.0, 1.0)
    parity = 1.0 - 2.0 * ((j[:, None] + j[None, :]) % 2)
    off = j[:, None] != j[None, :]
    gap = -2.0 * np.sin((phi[:, None] + phi[None, :]) / 2) * np.sin(
        (phi[:, None] - phi[None, :]) / 2
    )
    entries = np.where(off, c[:, None] / c[None, :] * parity / np.where(off, gap, 1.0), 0.0)
    entries = entries - np.diag(entries.sum(axis=1))
    slopes = np.sin(phi)[:, None] * entries / (R - 1)
    inverse = np.linalg.inv(slopes.T @ slopes + DIAG_SHIFT * np.eye(R))
    return slopes, inverse


def right_factor(matrix):
    high, low = split(np.asarray(matrix).T)
    half = np.concatenate([high, low], axis=1)
    return np.concatenate([half, half], axis=0)


def transform_tables():
    k = np.arange(FREQS)
    n = np.arange(NT)
    angle = 2.0 * math.pi * ((k[:, None] * n[None, :]) % NT) / NT
    table = np.stack([np.cos(angle), -np.sin(angle)])
    table = table.reshape(2, NF, PER, NT).transpose(0, 2, 1, 3).reshape(2 * FREQS, NT)
    inverse = np.concatenate(split(table.T / math.sqrt(FREQS)), axis=0)
    forward = np.concatenate(split(table / math.sqrt(NT)), axis=0)
    return inverse, forward


def halves(t):
    high = t.astype(jnp.bfloat16)
    low = (t - high.astype(jnp.float32)).astype(jnp.bfloat16)
    return jnp.concatenate([high, low], axis=1)


def along_radii(t, factor):
    both = jnp.dot(halves(t), factor, preferred_element_type=jnp.float32)
    return both[:, :R] + both[:, R:]


def transformed(table, t, rows):
    quad = jnp.dot(table, halves(t), preferred_element_type=jnp.float32)
    return (quad[:rows, :R] + quad[rows:, :R]) + (quad[:rows, R:] + quad[rows:, R:])


def march_kernel(
    az_ref, om_ref, state_ref, sedge_ref, force_ref, fedge_ref,
    plane_ref, pedge_ref, shape_ref, q_ref, send_ref, it_ref, b_ref, w_ref
):
    for n in range(AZ):
        w_ref[pl.ds(HALO + az_ref[n], NV, stride=EXT), :] = plane_ref[pl.ds(n * NV, NV), :]
    for v in range(NV):
        at = v * 2 * HALO
        w_ref[pl.ds(v * EXT, HALO), :] = pedge_ref[pl.ds(at + HALO, HALO), :]
        w_ref[pl.ds(v * EXT + HALO + AZ, HALO), :] = pedge_ref[pl.ds(at, HALO), :]
    for v in range(NV):
        rows = pl.ds(v * EXT, EXT)
        w_ref[rows, :] = w_ref[rows, :] * shape_ref[...]
    for c in range(NC):
        at = GUARD + c * EXT
        own = pl.ds(c * AZ, AZ)
        head = pl.ds(c * 2 * HALO, HALO)
        tail = pl.ds(c * 2 * HALO + HALO, HALO)
        for lo, size, part, ref, add_ref in (
            (0, HALO, tail, sedge_ref, fedge_ref),
            (HALO, AZ, own, state_ref, force_ref),
            (HALO + AZ, HALO, head, sedge_ref, fedge_ref),
        ):
            q = ref[part, :]
            it_ref[0, pl.ds(at + lo, size), :] = q
            b_ref[pl.ds(c * EXT + lo, size), :] = MARCH_WEIGHT * q + add_ref[part, :]

    factor = q_ref[...]

    def sweep(step, carry):
        now = lax.rem(step, 2)
        new = 1 - now
        for v in range(NV):
            w = w_ref[pl.ds(v * EXT, EXT), :]
            terms = [None] * 4
            for j in range(PER):
                rate = om_ref[j]
                planes = (j * NV + v, (PER + j) * NV + v)
                re, im = (it_ref[now, pl.ds(GUARD + c * EXT, EXT), :] for c in planes)
                for part, (c, mixed) in enumerate(
                    ((planes[0], w * re - rate * im), (planes[1], w * im + rate * re))
                ):
                    beside = (
                        it_ref[now, pl.ds(GUARD + c * EXT + 1, EXT), :]
                        + it_ref[now, pl.ds(GUARD + c * EXT - 1, EXT), :]
                    )
                    terms[part * PER + j] = (
                        b_ref[pl.ds(c * EXT, EXT), :] - mixed + SIDE_WEIGHT * beside
                    )
            done = along_radii(jnp.concatenate(terms, axis=0), factor)
            for i in range(4):
                it_ref[new, pl.ds(GUARD + (i * NV + v) * EXT, EXT), :] = done[
                    i * EXT : (i + 1) * EXT
                ]
        return carry

    lax.fori_loop(0, SWEEPS, sweep, 0)
    final = it_ref.at[0]
    for f in range(NF):
        send_ref[pl.ds(f * NC, NC), :] = final[
            pl.ds(GUARD + HALO + az_ref[f], NC, stride=EXT), :
        ]


def rows_of(v, size):
    return pl.ds(pl.multiple_of(v * size, size), size)


def unpack_kernel(points_ref, table_ref, *out_refs):
    table = table_ref[...]
    count = len(CHUNKS)
    for vs, x_ref, u_ref in zip(CHUNKS, out_refs[:count], out_refs[count:]):

        def one(at, carry, first=vs[0], x_ref=x_ref, u_ref=u_ref):
            x = jnp.concatenate(
                [
                    points_ref[pl.ds(i * NV + first + at, NF, stride=NC), :]
                    for i in range(2 * PER)
                ],
                axis=0,
            )
            x_ref[rows_of(at, KEPT), :] = x
            u_ref[rows_of(at, NT), :] = transformed(table, x, NT)
            return carry

        lax.fori_loop(0, len(vs), one, 0)


def radial_kernel(first, *refs):
    lead_ref, u_ref = (refs[0], refs[0]) if first else refs[:2]
    slope_ref, out_ref = refs[-2:]
    factor = slope_ref[...]
    u1 = lead_ref[pl.ds(NT, NT), :]
    for at in range(u_ref.shape[0] // NT):
        ur = along_radii(u_ref[pl.ds(at * NT, NT), :], factor)
        out_ref[pl.ds(at * NT, NT), :] = -ADVECT_SCALE * (u1 * ur)
        if first and at == 1:
            out_ref[pl.ds(0, NT), :] = out_ref[pl.ds(0, NT), :] - ADVECT_SCALE * (
                lead_ref[pl.ds(0, NT), :] * ur
            )


def sweep_rows(q, b, beside, w, rate, factor):
    re, im = q[:FREQS], q[FREQS:]
    mixed = jnp.concatenate([w * re - rate * im, w * im + rate * re], axis=0)
    return along_radii(b - mixed + SIDE_WEIGHT * beside, factor)


def rates():
    row = lax.broadcasted_iota(jnp.int32, (FREQS, R), 0)
    return (PER * (row & (NF - 1)) + (row >> 7)).astype(jnp.float32) * (0.5 / FREQS)


def forcing_kernel(
    first, lead_ref, part_ref, x_ref, next_ref, prev_ref, w_ref, inv_ref, fwd_ref, q_ref,
    new_ref, b_ref, *around_ref
):
    inverse, forward, factor = inv_ref[...], fwd_ref[...], q_ref[...]
    rate = rates()

    def around(v):
        rows = rows_of(v, KEPT)
        return transformed(inverse, 0.5 * (next_ref[rows, :] - prev_ref[rows, :]), NT)

    if first:
        around_ref[0][...] = around(2)

    def one(at, carry):
        rows, times = rows_of(at, KEPT), rows_of(at, NT)
        n = part_ref[times, :] - ADVECT_SCALE * (lead_ref[pl.ds(2 * NT, NT), :] * around(at))
        if first:
            extra = jnp.where(at == 0, ADVECT_SCALE, 0.0)
            n = n - extra * (lead_ref[pl.ds(0, NT), :] * around_ref[0][...])
        x = x_ref[rows, :]
        b = MARCH_WEIGHT * x + transformed(forward, n, KEPT)
        b_ref[rows, :] = b
        beside = next_ref[rows, :] + prev_ref[rows, :]
        new_ref[rows, :] = sweep_rows(x, b, beside, w_ref[pl.ds(at, 1), :], rate, factor)
        return carry

    lax.fori_loop(0, x_ref.shape[0] // KEPT, one, 0)


def sweep_kernel(x_ref, next_ref, prev_ref, b_ref, w_ref, q_ref, *more):
    factor = q_ref[...]
    rate = rates()
    new_ref = more[-2] if len(more) > 1 else more[-1]

    def one(at, carry):
        rows = rows_of(at, KEPT)
        beside = next_ref[rows, :] + prev_ref[rows, :]
        x = sweep_rows(
            x_ref[rows, :], b_ref[rows, :], beside, w_ref[pl.ds(at, 1), :], rate, factor
        )
        new_ref[rows, :] = x
        if len(more) > 1:
            more[-1][rows_of(at, NT), :] = transformed(more[0][...], x, NT)
        return carry

    lax.fori_loop(0, x_ref.shape[0] // KEPT, one, 0)


def pack_kernel(*refs):
    send_ref = refs[-1]
    for vs, x_ref in zip(CHUNKS, refs):
        for at, v in enumerate(vs):
            for i in range(2 * PER):
                send_ref[pl.ds(i * NV + v, NF, stride=2 * NC), :] = x_ref[
                    pl.ds(at * KEPT + i * NF, NF), :
                ]


def to_freq_kernel(*refs):
    count = len(CHUNKS)
    u_ref, fwd_ref, out_ref = refs[0], refs[-3], refs[-1]
    forward = fwd_ref[...]
    u2 = u_ref[pl.ds(2 * NT, NT), :]
    lead_next, lead_prev = refs[1 + count], refs[1 + 2 * count]
    for n, vs in enumerate(CHUNKS):
        part_ref, next_ref, prev_ref = (refs[1 + n + m * count] for m in range(3))

        def one(at, carry, first=vs[0], part=part_ref, ahead=next_ref, behind=prev_ref):
            rows = rows_of(at, NT)
            n = part[rows, :] - ADVECT_SCALE * (u2 * (0.5 * (ahead[rows, :] - behind[rows, :])))
            if first == 0:
                two = pl.ds(2 * NT, NT)
                around = 0.5 * (lead_next[two, :] - lead_prev[two, :])
                extra = jnp.where(at == 0, ADVECT_SCALE, 0.0)
                n = n - extra * (u_ref[pl.ds(0, NT), :] * around)
            g = transformed(forward, n, KEPT)
            for i in range(2 * PER):
                out_ref[pl.ds(NC + i * NV + first + at, NF, stride=2 * NC), :] = g[
                    i * NF : (i + 1) * NF
                ]
            return carry

        lax.fori_loop(0, len(vs), one, 0)


def place_kernel(az_ref, got_ref, state_ref, forcing_ref):
    for f in range(NF):
        to = pl.ds(az_ref[f], NC, stride=AZ)
        state_ref[to, :] = got_ref[pl.ds(f * 2 * NC, NC), :]
        forcing_ref[to, :] = got_ref[pl.ds(f * 2 * NC + NC, NC), :]


def sort_kernel(az_ref, plane_ref, out_ref):
    for n in range(AZ):
        out_ref[pl.ds(n * NV, NV), :] = plane_ref[pl.ds(az_ref[n], NV, stride=AZ), :]


def rim_kernel(at_ref, plane_ref, out_ref):
    for e in range(2 * HALO):
        out_ref[pl.ds(e, NV, stride=2 * HALO), :] = plane_ref[pl.ds(at_ref[e] * NV, NV), :]


ANY = pl.BlockSpec(memory_space=pl.ANY)
VMEM = pl.BlockSpec(memory_space=pltpu.VMEM)
SMEM = pl.BlockSpec(memory_space=pltpu.SMEM)


def call(kernel, specs, rows, name, work, scratch=(), aliases=None):
    shapes = [jax.ShapeDtypeStruct((n, R), jnp.float32) for n in rows]
    return pl.pallas_call(
        kernel,
        in_specs=specs,
        out_specs=[VMEM] * len(rows) if len(rows) > 1 else VMEM,
        out_shape=shapes if len(rows) > 1 else shapes[0],
        scratch_shapes=list(scratch),
        input_output_aliases=aliases or {},
        compiler_params=pltpu.CompilerParams(vmem_limit_bytes=32 << 20),
        cost_estimate=pl.CostEstimate(
            flops=int(work * 3e10), bytes_accessed=int(work * COST), transcendentals=0
        ),
        name=name,
    )


def exchange(blocks):
    return lax.all_to_all(
        blocks.reshape(NF, NV, 4, R), "freq", split_axis=0, concat_axis=0, tiled=True
    ).reshape(NF * NC, R)


def group_exchange(blocks, groups):
    return lax.all_to_all(
        blocks, "freq", split_axis=0, concat_axis=0, tiled=True, axis_index_groups=groups
    )


def neighbours(x):
    axes = ("freq", "plane")
    return lax.ppermute(x, axes, TO_PREV), lax.ppermute(x, axes, TO_NEXT)


def swapped(x):
    return lax.ppermute(x, "plane", [(0, 1), (1, 0)])


def edges(planes):
    planes = planes.reshape(NC, AZ, R)
    mine = jnp.concatenate([planes[:, :HALO], planes[:, AZ - HALO :]], axis=1)
    return swapped(mine.reshape(-1, R))


def fetch_planes(ordered, station_index, edge_at):
    held = group_exchange(ordered.reshape(16, 8 * NV, R), FLAT)
    mine = jnp.concatenate(
        [
            lax.dynamic_slice_in_dim(held, station_index[s] // 8, 1, axis=0)
            for s in range(STEPS)
        ],
        axis=0,
    )
    came = group_exchange(
        jnp.broadcast_to(mine.reshape(1, -1, R), (8, STEPS * 8 * NV, R)), TALL
    ).reshape(8, STEPS, 8 * NV, R)
    chosen = [
        lax.dynamic_index_in_dim(came[:, s], station_index[s] % 8, 0, keepdims=False)
        for s in range(STEPS)
    ]
    spread = group_exchange(jnp.broadcast_to(chosen[0][None], (16, 8 * NV, R)), FLAT)
    spread = spread.reshape(AZ * NV, R)
    rim = swapped(
        call(rim_kernel, [SMEM, VMEM], (NV * 2 * HALO,), "rim", 0.1)(edge_at, spread)
    )
    own = lax.dynamic_index_in_dim(
        chosen[1].reshape(8, NV, R), lax.axis_index("freq") % 8, 0, keepdims=False
    )
    return spread, rim, own


def per_device(state_in, forcing_in, base_flow, station_index, lobe_count):
    slopes, inverse_p = radial_tables()
    solve = jnp.asarray(right_factor(inverse_p))
    slope = jnp.asarray(right_factor(slopes))
    inverse, forward = (jnp.asarray(t) for t in transform_tables())
    f = lax.axis_index("freq")
    p = lax.axis_index("plane")

    def of_plane(table):
        return jnp.where(p == 0, jnp.asarray(table[0]), jnp.asarray(table[1]))

    az_of, edge_at = of_plane(AZ_OF), of_plane(EDGE_AT)
    omegas = 0.5 * (f * PER + jnp.arange(PER)).astype(jnp.float32) / FREQS

    def shaped(position):
        phases = lobe_count[0] * position % ALL_AZ
        chevron = 1.0 + 0.5 * jnp.cos(2.0 * math.pi * phases.astype(jnp.float32) / ALL_AZ)
        return BASE_SCALE * chevron

    shape_az = shaped((p * AZ - HALO + jnp.arange(EXT) + ALL_AZ) % ALL_AZ)
    shape_az = jnp.broadcast_to(shape_az[:, None], (EXT, R))

    state = state_in.reshape(NC * AZ, R)
    forcing = forcing_in.reshape(NC * AZ, R)
    ordered = call(sort_kernel, [SMEM, VMEM], (AZ * NV,), "sort", 1)(
        az_of, base_flow.reshape(NV * AZ, R)
    )
    ordered, state, forcing = lax.optimization_barrier((ordered, state, forcing))
    spread, rim, own = fetch_planes(ordered, station_index, edge_at)
    weight = own * shaped(p * AZ + az_of[f])

    send = call(
        march_kernel,
        [SMEM] * 2 + [VMEM] * 8,
        (NC * AZ,),
        "march",
        6,
        (
            pltpu.VMEM((2, NC * EXT + 2 * GUARD, R), jnp.float32),
            pltpu.VMEM((NC * EXT, R), jnp.float32),
            pltpu.VMEM((NV * EXT, R), jnp.float32),
        ),
    )(
        az_of, omegas, state, edges(state), forcing, edges(forcing),
        spread, rim, shape_az, solve,
    )
    counts = [len(vs) for vs in CHUNKS]
    weights = [
        jnp.pad(weight[vs[0] : vs[-1] + 1], ((0, 8 - len(vs)), (0, 0))) for vs in CHUNKS
    ]

    def radial(us):
        return [
            call(
                lambda *refs, first=n == 0: radial_kernel(first, *refs),
                [VMEM] * (2 if n == 0 else 3),
                (counts[n] * NT,),
                "radial",
                0.01,
            )(*((u,) if n == 0 else (us[0], u)), slope)
            for n, u in enumerate(us)
        ]

    unpacked = call(
        unpack_kernel,
        [VMEM] * 2,
        [n * KEPT for n in counts] + [n * NT for n in counts],
        "unpack",
        2,
    )(exchange(send), inverse)
    xs, us = list(unpacked[: len(counts)]), list(unpacked[len(counts) :])
    sides = []
    for n, x in enumerate(xs):
        if sides:
            x, sides[-1] = lax.optimization_barrier((x, sides[-1]))
        sides.append(neighbours(x))
    parts = radial(us)
    bs = []
    before = xs[0]
    for n, x in enumerate(xs):
        xs[n], b = call(
            lambda _, *refs, first=n == 0: forcing_kernel(first, *refs),
            [ANY] + [VMEM] * 9,
            (counts[n] * KEPT,) * 2,
            "forcing",
            counts[n],
            (pltpu.VMEM((NT, R), jnp.float32),) if n == 0 else (),
        )(before, us[0], parts[n], x, *sides[n], weights[n], inverse, forward, solve)
        before = xs[n]
        bs.append(b)
        sides[n] = neighbours(xs[n])
    for sweep in range(1, SWEEPS):
        last = sweep == SWEEPS - 1
        for n, x in enumerate(xs):
            done = call(
                lambda _, *refs: sweep_kernel(*refs),
                [ANY] + [VMEM] * (7 if last else 6),
                (counts[n] * KEPT,) + ((counts[n] * NT,) if last else ()),
                "sweep",
                (0.7 if last else 0.3) * counts[n],
            )(before, x, *sides[n], bs[n], weights[n], solve, *((inverse,) if last else ()))
            if last:
                xs[n], us[n] = done
                sides[n] = neighbours(us[n])
            else:
                xs[n] = done
                sides[n] = neighbours(done)
            before = xs[n]
    packed = call(pack_kernel, [VMEM] * len(xs), (2 * NC * AZ,), "pack", 0.01)(*xs)
    parts = radial(us)
    operands = (
        us[0], *parts, *[s[0] for s in sides], *[s[1] for s in sides], forward, packed
    )
    back = call(
        to_freq_kernel,
        [VMEM] * len(operands),
        (2 * NC * AZ,),
        "to_freq",
        2.5,
        aliases={len(operands) - 1: 0},
    )(*operands)
    got = lax.all_to_all(
        back.reshape(NF, 2 * NC, R), "freq", split_axis=0, concat_axis=0, tiled=True
    ).reshape(-1, R)
    state, forcing = call(place_kernel, [SMEM, VMEM], (NC * AZ,) * 2, "place", 4)(az_of, got)
    return (state.reshape(state_in.shape), forcing.reshape(state_in.shape))


def solution(mesh):
    return jax.shard_map(
        per_device,
        mesh=mesh,
        in_specs=(
            P(None, "freq", None, "plane", None),
            P(None, "freq", None, "plane", None),
            P("freq", None, "plane", None),
            P(),
            P(),
        ),
        out_specs=(P(None, "freq", None, "plane", None), P(None, "freq", None, "plane", None)),
        check_vma=False,
    )
```

```python
import itertools
import math

import jax
import jax.numpy as jnp
import numpy as np
from jax import lax
from jax.experimental import pallas as pl
from jax.experimental.pallas import tpu as pltpu
from jax.sharding import PartitionSpec as P

SWEEPS = 4
STEPS = 2
SIDE_WEIGHT = 1.25
MARCH_WEIGHT = 4.0
DIAG_SHIFT = 4.0
ADVECT_SCALE = 0.5
BASE_SCALE = 0.5

NF = 128
PER = 2
NV = 5
AZ = 128
ALL_AZ = 256
R = 128
FREQS = NF * PER
NT = 3 * FREQS // 2
NC = 2 * PER * NV
HALO = 4
EXT = AZ + 2 * HALO
GUARD = 8
KEPT = 2 * FREQS
CHUNKS = ((0, 1, 2), (3, 4))
COST = 1e8


def freq_index(x, y, z, c):
    return ((x * 4 + y) * 4 + z) * 2 + c


def ring_orders():
    snake = [
        (x, y) for y in range(4) for x in (range(4) if y % 2 == 0 else range(3, -1, -1))
    ]
    cycle = [(0, 0), (1, 0), (2, 0), (3, 0), (3, 1), (3, 2), (3, 3), (2, 3)]
    cycle += [(2, 2), (2, 1), (1, 1), (1, 2), (1, 3), (0, 3), (0, 2), (0, 1)]

    def walk(start, end):
        i = cycle.index(start)
        forward = cycle[i:] + cycle[:i]
        if forward[-1] == end:
            return forward
        return [cycle[i]] + cycle[:i][::-1] + cycle[i + 1 :][::-1]

    first = []
    for z in range(4):
        first += [(x, y, z) for x, y in (snake if z % 2 == 0 else snake[::-1])]
    second = [(y, x, 3) for x, y in snake]
    second += [(x, y, 2) for x, y in walk((3, 0), (2, 0))]
    second += [(x, y, 1) for x, y in walk((2, 0), (1, 0))]
    second += [(x, y, 0) for x, y in walk((1, 0), (0, 0))]
    return [
        [freq_index(x, y, z, c) for x, y, z in path for c in (0, 1)]
        for path in (first, second)
    ]


ORDERS = ring_orders()
AZ_OF = np.argsort(np.array(ORDERS), axis=1).astype(np.int32)
RING = [f * 2 + p for p in (0, 1) for f in ORDERS[p]]
TO_NEXT = [(RING[i], RING[(i + 1) % ALL_AZ]) for i in range(ALL_AZ)]
TO_PREV = [(RING[(i + 1) % ALL_AZ], RING[i]) for i in range(ALL_AZ)]
FLAT = [[g * 8 + s for g in range(16)] for s in range(8)]
TALL = [[g * 8 + s for s in range(8)] for g in range(16)]
EDGE_AT = np.array(
    [[ORDERS[p][a] for a in (*range(HALO), *range(AZ - HALO, AZ))] for p in (0, 1)], np.int32
)


def split(table):
    table = np.asarray(table, np.float32)
    high = table.astype(jnp.bfloat16)
    low = (table - high.astype(np.float32)).astype(jnp.bfloat16)
    return high, low


def radial_tables():
    j = np.arange(R)
    phi = math.pi * j / (R - 1)
    x = np.cos(phi)
    c = np.where((j == 0) | (j == R - 1), 2.0, 1.0)
    parity = 1.0 - 2.0 * ((j[:, None] + j[None, :]) % 2)
    off = j[:, None] != j[None, :]
    gap = -2.0 * np.sin((phi[:, None] + phi[None, :]) / 2) * np.sin(
        (phi[:, None] - phi[None, :]) / 2
    )
    entries = np.where(off, c[:, None] / c[None, :] * parity / np.where(off, gap, 1.0), 0.0)
    entries = entries - np.diag(entries.sum(axis=1))
    slopes = np.sin(phi)[:, None] * entries / (R - 1)
    inverse = np.linalg.inv(slopes.T @ slopes + DIAG_SHIFT * np.eye(R))
    return slopes, inverse


def right_factor(matrix):
    high, low = split(np.asarray(matrix).T)
    half = np.concatenate([high, low], axis=1)
    return np.concatenate([half, half], axis=0)


def transform_tables():
    k = np.arange(FREQS)
    n = np.arange(NT)
    angle = 2.0 * math.pi * ((k[:, None] * n[None, :]) % NT) / NT
    table = np.stack([np.cos(angle), -np.sin(angle)])
    table = table.reshape(2, NF, PER, NT).transpose(0, 2, 1, 3).reshape(2 * FREQS, NT)
    inverse = np.concatenate(split(table.T / math.sqrt(FREQS)), axis=0)
    forward = np.concatenate(split(table / math.sqrt(NT)), axis=0)
    return inverse, forward


def halves(t):
    high = t.astype(jnp.bfloat16)
    low = (t - high.astype(jnp.float32)).astype(jnp.bfloat16)
    return jnp.concatenate([high, low], axis=1)


def along_radii(t, factor):
    both = jnp.dot(halves(t), factor, preferred_element_type=jnp.float32)
    return both[:, :R] + both[:, R:]


def transformed(table, t, rows):
    quad = jnp.dot(table, halves(t), preferred_element_type=jnp.float32)
    return (quad[:rows, :R] + quad[rows:, :R]) + (quad[:rows, R:] + quad[rows:, R:])


def march_kernel(
    az_ref, om_ref, state_ref, sedge_ref, force_ref, fedge_ref,
    plane_ref, pedge_ref, shape_ref, q_ref, send_ref, it_ref, b_ref, w_ref
):
    for n in range(AZ):
        w_ref[pl.ds(HALO + az_ref[n], NV, stride=EXT), :] = plane_ref[pl.ds(n * NV, NV), :]
    for v in range(NV):
        at = v * 2 * HALO
        w_ref[pl.ds(v * EXT, HALO), :] = pedge_ref[pl.ds(at + HALO, HALO), :]
        w_ref[pl.ds(v * EXT + HALO + AZ, HALO), :] = pedge_ref[pl.ds(at, HALO), :]
    for v in range(NV):
        rows = pl.ds(v * EXT, EXT)
        w_ref[rows, :] = w_ref[rows, :] * shape_ref[...]
    for c in range(NC):
        at = GUARD + c * EXT
        own = pl.ds(c * AZ, AZ)
        head = pl.ds(c * 2 * HALO, HALO)
        tail = pl.ds(c * 2 * HALO + HALO, HALO)
        for lo, size, part, ref, add_ref in (
            (0, HALO, tail, sedge_ref, fedge_ref),
            (HALO, AZ, own, state_ref, force_ref),
            (HALO + AZ, HALO, head, sedge_ref, fedge_ref),
        ):
            q = ref[part, :]
            it_ref[0, pl.ds(at + lo, size), :] = q
            b_ref[pl.ds(c * EXT + lo, size), :] = MARCH_WEIGHT * q + add_ref[part, :]

    factor = q_ref[...]

    def sweep(step, carry):
        now = lax.rem(step, 2)
        new = 1 - now
        for v in range(NV):
            w = w_ref[pl.ds(v * EXT, EXT), :]
            terms = [None] * 4
            for j in range(PER):
                rate = om_ref[j]
                planes = (j * NV + v, (PER + j) * NV + v)
                re, im = (it_ref[now, pl.ds(GUARD + c * EXT, EXT), :] for c in planes)
                for part, (c, mixed) in enumerate(
                    ((planes[0], w * re - rate * im), (planes[1], w * im + rate * re))
                ):
                    beside = (
                        it_ref[now, pl.ds(GUARD + c * EXT + 1, EXT), :]
                        + it_ref[now, pl.ds(GUARD + c * EXT - 1, EXT), :]
                    )
                    terms[part * PER + j] = (
                        b_ref[pl.ds(c * EXT, EXT), :] - mixed + SIDE_WEIGHT * beside
                    )
            done = along_radii(jnp.concatenate(terms, axis=0), factor)
            for i in range(4):
                it_ref[new, pl.ds(GUARD + (i * NV + v) * EXT, EXT), :] = done[
                    i * EXT : (i + 1) * EXT
                ]
        return carry

    lax.fori_loop(0, SWEEPS, sweep, 0)
    final = it_ref.at[0]
    for f in range(NF):
        send_ref[pl.ds(f * NC, NC), :] = final[
            pl.ds(GUARD + HALO + az_ref[f], NC, stride=EXT), :
        ]


def rows_of(v, size):
    return pl.ds(pl.multiple_of(v * size, size), size)


def unpack_kernel(points_ref, table_ref, *out_refs):
    table = table_ref[...]
    count = len(CHUNKS)
    for vs, x_ref, u_ref in zip(CHUNKS, out_refs[:count], out_refs[count:]):

        def one(at, carry, first=vs[0], x_ref=x_ref, u_ref=u_ref):
            x = jnp.concatenate(
                [
                    points_ref[pl.ds(i * NV + first + at, NF, stride=NC), :]
                    for i in range(2 * PER)
                ],
                axis=0,
            )
            x_ref[rows_of(at, KEPT), :] = x
            u_ref[rows_of(at, NT), :] = transformed(table, x, NT)
            return carry

        lax.fori_loop(0, len(vs), one, 0)


def radial_kernel(first, *refs):
    lead_ref, u_ref = (refs[0], refs[0]) if first else refs[:2]
    slope_ref, out_ref = refs[-2:]
    factor = slope_ref[...]
    u1 = lead_ref[pl.ds(NT, NT), :]
    for at in range(u_ref.shape[0] // NT):
        ur = along_radii(u_ref[pl.ds(at * NT, NT), :], factor)
        out_ref[pl.ds(at * NT, NT), :] = -ADVECT_SCALE * (u1 * ur)
        if first and at == 1:
            out_ref[pl.ds(0, NT), :] = out_ref[pl.ds(0, NT), :] - ADVECT_SCALE * (
                lead_ref[pl.ds(0, NT), :] * ur
            )


def sweep_rows(q, b, beside, w, rate, factor):
    re, im = q[:FREQS], q[FREQS:]
    mixed = jnp.concatenate([w * re - rate * im, w * im + rate * re], axis=0)
    return along_radii(b - mixed + SIDE_WEIGHT * beside, factor)


def rates():
    row = lax.broadcasted_iota(jnp.int32, (FREQS, R), 0)
    return (PER * (row & (NF - 1)) + (row >> 7)).astype(jnp.float32) * (0.5 / FREQS)


def forcing_kernel(
    first, lead_ref, part_ref, x_ref, next_ref, prev_ref, w_ref, inv_ref, fwd_ref, q_ref,
    new_ref, b_ref, *around_ref
):
    inverse, forward, factor = inv_ref[...], fwd_ref[...], q_ref[...]
    rate = rates()

    def around(v):
        rows = rows_of(v, KEPT)
        return transformed(inverse, 0.5 * (next_ref[rows, :] - prev_ref[rows, :]), NT)

    if first:
        around_ref[0][...] = around(2)

    def one(at, carry):
        rows, times = rows_of(at, KEPT), rows_of(at, NT)
        n = part_ref[times, :] - ADVECT_SCALE * (lead_ref[pl.ds(2 * NT, NT), :] * around(at))
        if first:
            extra = jnp.where(at == 0, ADVECT_SCALE, 0.0)
            n = n - extra * (lead_ref[pl.ds(0, NT), :] * around_ref[0][...])
        x = x_ref[rows, :]
        b = MARCH_WEIGHT * x + transformed(forward, n, KEPT)
        b_ref[rows, :] = b
        beside = next_ref[rows, :] + prev_ref[rows, :]
        new_ref[rows, :] = sweep_rows(x, b, beside, w_ref[pl.ds(at, 1), :], rate, factor)
        return carry

    lax.fori_loop(0, x_ref.shape[0] // KEPT, one, 0)


def sweep_kernel(x_ref, next_ref, prev_ref, b_ref, w_ref, q_ref, *more):
    factor = q_ref[...]
    rate = rates()
    new_ref = more[-2] if len(more) > 1 else more[-1]

    def one(at, carry):
        rows = rows_of(at, KEPT)
        beside = next_ref[rows, :] + prev_ref[rows, :]
        x = sweep_rows(
            x_ref[rows, :], b_ref[rows, :], beside, w_ref[pl.ds(at, 1), :], rate, factor
        )
        new_ref[rows, :] = x
        if len(more) > 1:
            more[-1][rows_of(at, NT), :] = transformed(more[0][...], x, NT)
        return carry

    lax.fori_loop(0, x_ref.shape[0] // KEPT, one, 0)


def pack_kernel(*refs):
    send_ref = refs[-1]
    for vs, x_ref in zip(CHUNKS, refs):
        for at, v in enumerate(vs):
            for i in range(2 * PER):
                send_ref[pl.ds(i * NV + v, NF, stride=2 * NC), :] = x_ref[
                    pl.ds(at * KEPT + i * NF, NF), :
                ]


def to_freq_kernel(*refs):
    count = len(CHUNKS)
    u_ref, fwd_ref, out_ref = refs[0], refs[-3], refs[-1]
    forward = fwd_ref[...]
    u2 = u_ref[pl.ds(2 * NT, NT), :]
    lead_next, lead_prev = refs[1 + count], refs[1 + 2 * count]
    for n, vs in enumerate(CHUNKS):
        part_ref, next_ref, prev_ref = (refs[1 + n + m * count] for m in range(3))

        def one(at, carry, first=vs[0], part=part_ref, ahead=next_ref, behind=prev_ref):
            rows = rows_of(at, NT)
            n = part[rows, :] - ADVECT_SCALE * (u2 * (0.5 * (ahead[rows, :] - behind[rows, :])))
            if first == 0:
                two = pl.ds(2 * NT, NT)
                around = 0.5 * (lead_next[two, :] - lead_prev[two, :])
                extra = jnp.where(at == 0, ADVECT_SCALE, 0.0)
                n = n - extra * (u_ref[pl.ds(0, NT), :] * around)
            g = transformed(forward, n, KEPT)
            for i in range(2 * PER):
                out_ref[pl.ds(NC + i * NV + first + at, NF, stride=2 * NC), :] = g[
                    i * NF : (i + 1) * NF
                ]
            return carry

        lax.fori_loop(0, len(vs), one, 0)


def place_kernel(az_ref, got_ref, state_ref, forcing_ref):
    for f in range(NF):
        to = pl.ds(az_ref[f], NC, stride=AZ)
        state_ref[to, :] = got_ref[pl.ds(f * 2 * NC, NC), :]
        forcing_ref[to, :] = got_ref[pl.ds(f * 2 * NC + NC, NC), :]


def sort_kernel(az_ref, plane_ref, out_ref):
    for n in range(AZ):
        out_ref[pl.ds(n * NV, NV), :] = plane_ref[pl.ds(az_ref[n], NV, stride=AZ), :]


def rim_kernel(at_ref, plane_ref, out_ref):
    for e in range(2 * HALO):
        out_ref[pl.ds(e, NV, stride=2 * HALO), :] = plane_ref[pl.ds(at_ref[e] * NV, NV), :]


ANY = pl.BlockSpec(memory_space=pl.ANY)
VMEM = pl.BlockSpec(memory_space=pltpu.VMEM)
SMEM = pl.BlockSpec(memory_space=pltpu.SMEM)


def call(kernel, specs, rows, name, work, scratch=(), aliases=None):
    shapes = [jax.ShapeDtypeStruct((n, R), jnp.float32) for n in rows]
    return pl.pallas_call(
        kernel,
        in_specs=specs,
        out_specs=[VMEM] * len(rows) if len(rows) > 1 else VMEM,
        out_shape=shapes if len(rows) > 1 else shapes[0],
        scratch_shapes=list(scratch),
        input_output_aliases=aliases or {},
        compiler_params=pltpu.CompilerParams(vmem_limit_bytes=16 << 20),
        cost_estimate=pl.CostEstimate(
            flops=int(work * 3e10), bytes_accessed=int(work * COST), transcendentals=0
        ),
        name=name,
    )


def exchange(blocks):
    return lax.all_to_all(
        blocks.reshape(NF, NV, 4, R), "freq", split_axis=0, concat_axis=0, tiled=True
    ).reshape(NF * NC, R)


def group_exchange(blocks, groups):
    return lax.all_to_all(
        blocks, "freq", split_axis=0, concat_axis=0, tiled=True, axis_index_groups=groups
    )


def neighbours(x):
    axes = ("freq", "plane")
    return lax.ppermute(x, axes, TO_PREV), lax.ppermute(x, axes, TO_NEXT)


def swapped(x):
    return lax.ppermute(x, "plane", [(0, 1), (1, 0)])


def edges(planes):
    planes = planes.reshape(NC, AZ, R)
    mine = jnp.concatenate([planes[:, :HALO], planes[:, AZ - HALO :]], axis=1)
    return swapped(mine.reshape(-1, R))


def fetch_planes(ordered, station_index, edge_at, state, forcing):
    held = group_exchange(ordered.reshape(16, 8 * NV, R), FLAT)
    mine = [
        lax.dynamic_index_in_dim(held, station_index[s] // 8, 0, keepdims=False)
        for s in range(STEPS)
    ]
    block = jnp.concatenate(
        [
            jnp.broadcast_to(mine[0][None], (8, 8 * NV, R)),
            jnp.pad(mine[1].reshape(8, NV, R), ((0, 0), (0, 3), (0, 0))),
        ],
        axis=1,
    )
    came = group_exchange(block, TALL)
    came, state, forcing = lax.optimization_barrier((came, state, forcing))
    beside = edges(state), edges(forcing)
    chosen = lax.dynamic_index_in_dim(came, station_index[0] % 8, 0, keepdims=False)
    own = lax.dynamic_index_in_dim(came, station_index[1] % 8, 0, keepdims=False)
    spread = group_exchange(
        jnp.broadcast_to(chosen[None, : 8 * NV], (16, 8 * NV, R)), FLAT
    ).reshape(AZ * NV, R)
    rim = swapped(
        call(rim_kernel, [SMEM, VMEM], (NV * 2 * HALO,), "rim", 0.1)(edge_at, spread)
    )
    return spread, rim, own[8 * NV : 9 * NV], beside


def per_device(state_in, forcing_in, base_flow, station_index, lobe_count):
    slopes, inverse_p = radial_tables()
    solve = jnp.asarray(right_factor(inverse_p))
    slope = jnp.asarray(right_factor(slopes))
    inverse, forward = (jnp.asarray(t) for t in transform_tables())
    f = lax.axis_index("freq")
    p = lax.axis_index("plane")

    def of_plane(table):
        return jnp.where(p == 0, jnp.asarray(table[0]), jnp.asarray(table[1]))

    az_of, edge_at = of_plane(AZ_OF), of_plane(EDGE_AT)
    omegas = 0.5 * (f * PER + jnp.arange(PER)).astype(jnp.float32) / FREQS

    def shaped(position):
        phases = lobe_count[0] * position % ALL_AZ
        chevron = 1.0 + 0.5 * jnp.cos(2.0 * math.pi * phases.astype(jnp.float32) / ALL_AZ)
        return BASE_SCALE * chevron

    shape_az = shaped((p * AZ - HALO + jnp.arange(EXT) + ALL_AZ) % ALL_AZ)
    shape_az = jnp.broadcast_to(shape_az[:, None], (EXT, R))

    state = state_in.reshape(NC * AZ, R)
    forcing = forcing_in.reshape(NC * AZ, R)
    ordered = call(sort_kernel, [SMEM, VMEM], (AZ * NV,), "sort", 1)(
        az_of, base_flow.reshape(NV * AZ, R)
    )
    spread, rim, own, beside = fetch_planes(ordered, station_index, edge_at, state, forcing)
    weight = own * shaped(p * AZ + az_of[f])

    send = call(
        march_kernel,
        [SMEM] * 2 + [VMEM] * 8,
        (NC * AZ,),
        "march",
        6,
        (
            pltpu.VMEM((2, NC * EXT + 2 * GUARD, R), jnp.float32),
            pltpu.VMEM((NC * EXT, R), jnp.float32),
            pltpu.VMEM((NV * EXT, R), jnp.float32),
        ),
    )(
        az_of, omegas, state, beside[0], forcing, beside[1],
        spread, rim, shape_az, solve,
    )
    counts = [len(vs) for vs in CHUNKS]
    weights = [
        jnp.pad(weight[vs[0] : vs[-1] + 1], ((0, 8 - len(vs)), (0, 0))) for vs in CHUNKS
    ]

    def radial(us):
        return [
            call(
                lambda *refs, first=n == 0: radial_kernel(first, *refs),
                [VMEM] * (2 if n == 0 else 3),
                (counts[n] * NT,),
                "radial",
                0.01,
            )(*((u,) if n == 0 else (us[0], u)), slope)
            for n, u in enumerate(us)
        ]

    unpacked = call(
        unpack_kernel,
        [VMEM] * 2,
        [n * KEPT for n in counts] + [n * NT for n in counts],
        "unpack",
        2,
    )(exchange(send), inverse)
    xs, us = list(unpacked[: len(counts)]), list(unpacked[len(counts) :])
    sides = []
    for n, x in enumerate(xs):
        if sides:
            x, sides[-1] = lax.optimization_barrier((x, sides[-1]))
        sides.append(neighbours(x))
    parts = radial(us)
    bs = []
    before = xs[0]
    for n, x in enumerate(xs):
        xs[n], b = call(
            lambda _, *refs, first=n == 0: forcing_kernel(first, *refs),
            [ANY] + [VMEM] * 9,
            (counts[n] * KEPT,) * 2,
            "forcing",
            counts[n],
            (pltpu.VMEM((NT, R), jnp.float32),) if n == 0 else (),
        )(before, us[0], parts[n], x, *sides[n], weights[n], inverse, forward, solve)
        before = xs[n]
        bs.append(b)
        sides[n] = neighbours(xs[n])
    for sweep in range(1, SWEEPS):
        last = sweep == SWEEPS - 1
        for n, x in enumerate(xs):
            done = call(
                lambda _, *refs: sweep_kernel(*refs),
                [ANY] + [VMEM] * (7 if last else 6),
                (counts[n] * KEPT,) + ((counts[n] * NT,) if last else ()),
                "sweep",
                (0.7 if last else 0.3) * counts[n],
            )(before, x, *sides[n], bs[n], weights[n], solve, *((inverse,) if last else ()))
            if last:
                xs[n], us[n] = done
                sides[n] = neighbours(us[n])
            else:
                xs[n] = done
                sides[n] = neighbours(done)
            before = xs[n]
    packed = call(pack_kernel, [VMEM] * len(xs), (2 * NC * AZ,), "pack", 0.01)(*xs)
    parts = radial(us)
    operands = (
        us[0], *parts, *[s[0] for s in sides], *[s[1] for s in sides], forward, packed
    )
    back = call(
        to_freq_kernel,
        [VMEM] * len(operands),
        (2 * NC * AZ,),
        "to_freq",
        2.5,
        aliases={len(operands) - 1: 0},
    )(*operands)
    got = lax.all_to_all(
        back.reshape(NF, 2 * NC, R), "freq", split_axis=0, concat_axis=0, tiled=True
    ).reshape(-1, R)
    state, forcing = call(place_kernel, [SMEM, VMEM], (NC * AZ,) * 2, "place", 4)(az_of, got)
    return (state.reshape(state_in.shape), forcing.reshape(state_in.shape))


def solution(mesh):
    return jax.shard_map(
        per_device,
        mesh=mesh,
        in_specs=(
            P(None, "freq", None, "plane", None),
            P(None, "freq", None, "plane", None),
            P("freq", None, "plane", None),
            P(),
            P(),
        ),
        out_specs=(P(None, "freq", None, "plane", None), P(None, "freq", None, "plane", None)),
        check_vma=False,
    )
```
